32 devices in a mesh: seq: 8 (over z, y), dp: 4 (over x, core).
Axes of the slice: x: 2, y: 2, z: 4, core: 2. Of those that a mesh axis runs over, the one named last changes fastest.
Arguments:
- conv_input: bfloat16 [4, 1024, 2816], P('dp', 'seq'), may hold values from -6 to 6
- dt_raw: bfloat16 [4, 1024, 40], P('dp', 'seq'), may hold values from -3 to 3
- packing: int32 [4, 32, 2], P('dp', 'seq'), may hold values from 0 to 3, as said below
- resets: int32 [4, 1024], P('dp', 'seq'), may hold values 0 or 1
- conv_weight: float32 [4, 2816], replicated, may hold values from -3 to 3
- conv_bias: float32 [2816], replicated, may hold values from -1.5 to 1.5
- dt_bias: float32 [40], replicated
- decay_rate: float32 [40], replicated, may hold values from 0.5 to 2
- skip_gain: float32 [40], replicated, may hold values from 0.5 to 1.5
- grad_out: bfloat16 [4, 1024, 2560], P('dp', 'seq'), may hold values from -6 to 6
Outputs:
- layer_out: bfloat16 [4, 1024, 2560], P('dp', 'seq')
- grad_input: bfloat16 [4, 1024, 2816], P('dp', 'seq')
- grad_dt_raw: bfloat16 [4, 1024, 40], P('dp', 'seq')
- grad_conv_weight: float32 [4, 2816], replicated
- grad_conv_bias: float32 [2816], replicated
- grad_dt_bias: float32 [40], replicated
- grad_decay_rate: float32 [40], replicated
- grad_skip_gain: float32 [40], replicated
The draws below stay inside these ranges and needn't reach their ends.
Inputs may be any that keep to these rules, and one draw needn't show every extreme that they name: `packing`: entry 0 names a packed sequence, entry 1 a block slot below 4. Within one shard, the 4 blocks of one loader row go to 4 distinct packed sequences, one to each, and each packed sequence receives exactly 4 blocks into distinct slots.
All inputs are finite; a program needn't handle non-finite values. No bound on the sum of `resets` on one device may be relied on, other than what follows from the above.
Results may differ from the reference program's by a relative error of at most 0.01.
Values may be sent and summed in bfloat16 or wider, within the bound.
A program may use at most 192 MiB of HBM per device.

```python
import math
import jax
import jax.numpy as jnp
from jax import lax

H = 40
P_SIZE = 64
N = 128
K = 4
Q = 128
BLK = 32
RB = 4
TOK_DEV = 128
SEQ_LEN = 1024
SEQS = 4
SEQ_BLOCKS = 32
CH = 2816


def draw_packing(key, part):
    shard_keys = jax.random.split(key, SEQ_BLOCKS // RB)

    def slot_order(slot_key):
        return jax.random.permutation(slot_key, RB)

    def one_shard(shard_key):
        first_key, second_key, third_key = jax.random.split(shard_key, 3)
        rotation = jax.random.permutation(first_key, SEQS)
        shifts = jax.random.permutation(second_key, SEQS)[:RB]
        slot_perm = jax.vmap(slot_order)(jax.random.split(third_key, SEQS))
        target = (rotation[:, None] + shifts[None, :]) % SEQS
        layers = jnp.arange(RB)
        slot_index = slot_perm[target, layers[None, :]]
        return jnp.stack([target, slot_index], axis=-1)
    per_shard = jax.vmap(one_shard)(shard_keys)
    return jnp.transpose(per_shard, (1, 0, 2, 3)).reshape(SEQS, SEQ_BLOCKS, 2).astype(jnp.int32)


def draw_dt_bias(key, part):
    lowest = -math.log(SEQ_LEN)
    highest = -math.log(30.0)
    return jax.random.uniform(key, (H,), jnp.float32, lowest, highest)


def set_ends(entries, key, least, top_value):
    longest = entries.shape.index(max(entries.shape))
    spots = []
    for shift in (0, 1):
        where = [jax.random.randint(jax.random.fold_in(key, axis), (), 0, length) for axis, length in enumerate(entries.shape)]
        where[longest] = (where[longest] + shift) % entries.shape[longest]
        spots.append(tuple(where))
    return entries.at[spots[0]].set(least).at[spots[1]].set(top_value)


def shard_levels(own_key, dims, shards, least, largest):
    def one(dim, parts):
        heights = jax.random.uniform(jax.random.fold_in(jax.random.fold_in(own_key, 6), dim), (parts,), jnp.float32, least / len(shards), largest / len(shards))
        return jnp.repeat(jnp.exp(heights), dims[dim] // parts).reshape((-1,) + (1,) * (len(dims) - dim - 1))

    loudness = one(*shards[0])
    for cut in shards[1:]:
        loudness = loudness * one(*cut)
    return loudness


def gaussian(own_key, extent, scale, bound, cuts=(), kind=jnp.bfloat16):
    factor_of = shard_levels(own_key, extent, cuts, -0.22, 0.18) if cuts else 1.0
    entries = jax.random.normal(own_key, extent, jnp.float32) * scale * factor_of
    return jnp.minimum(jnp.maximum(entries, -bound), bound).astype(kind)


def setup_inputs(seed: int = 0) -> dict:
    arg_keys = jax.random.split(jax.random.key(seed), 11)
    return {
        "conv_input": gaussian(arg_keys[0], (SEQS, SEQ_LEN, CH), 1.0, 6.0, ((0, 4), (1, 8))),
        "dt_raw": gaussian(arg_keys[1], (SEQS, SEQ_LEN, H), 0.5, 3.0, ((0, 4), (1, 8))),
        "packing": draw_packing(jax.random.fold_in(arg_keys[10], 71), 0),
        "resets": set_ends((jax.random.randint(arg_keys[3], (SEQS, SEQ_LEN), 0, TOK_DEV * 8) < 1).astype(jnp.int32), jax.random.fold_in(arg_keys[3], 1), 0, 1),
        "conv_weight": gaussian(arg_keys[4], (K, CH), K ** -0.5, 3.0, (), jnp.float32),
        "conv_bias": gaussian(arg_keys[5], (CH,), 0.3, 1.5, (), jnp.float32),
        "dt_bias": draw_dt_bias(jax.random.fold_in(arg_keys[10], 71), 0),
        "decay_rate": jnp.clip(jnp.exp(jax.random.uniform(arg_keys[7], (H,), jnp.float32, math.log(0.5), math.log(2.0))), 0.5, 2.0),
        "skip_gain": jnp.clip(jax.random.uniform(arg_keys[8], (H,), jnp.float32, 0.5, 1.5), 0.5, 1.5),
        "grad_out": gaussian(arg_keys[9], (SEQS, SEQ_LEN, H * P_SIZE), 1.0, 6.0, ((0, 4), (1, 8))),
    }


def contract(form, left, right):
    return jnp.einsum(form, left.astype(jnp.float32), right.astype(jnp.float32))

def conv_silu(row_data, prior_rows, prior_keep, keep_rows, conv_weight, conv_bias):
    n_taps = conv_weight.shape[0]
    length = row_data.shape[0]
    padded = jnp.concatenate([prior_rows, row_data], axis=0)
    keep_all = jnp.concatenate([prior_keep, keep_rows], axis=0)
    summed = conv_bias[None, :] + conv_weight[n_taps - 1][None, :] * row_data
    joined = jnp.ones((length,), jnp.float32)
    for offset in range(1, n_taps):
        joined = joined * keep_all[n_taps - offset:n_taps - offset + length]
        earlier = padded[n_taps - 1 - offset:n_taps - 1 - offset + length]
        summed = summed + conv_weight[n_taps - 1 - offset][None, :] * earlier * joined[:, None]
    return jax.nn.silu(summed).astype(jnp.bfloat16)

def step_sizes(step_raw, dt_bias, decay_rate):
    step_size = jax.nn.softplus(step_raw + dt_bias[None, :])
    return (step_size, -step_size * decay_rate[None, :])

def split_inputs(activated, step_size, n_heads, head_size, n_state):
    inner_width = n_heads * head_size
    inputs_x = activated[..., :inner_width].reshape(activated.shape[:-1] + (n_heads, head_size))
    b_rows = activated[..., inner_width:inner_width + n_state]
    c_rows = activated[..., inner_width + n_state:]
    x_scaled = (inputs_x.astype(jnp.float32) * step_size[..., None]).astype(jnp.bfloat16)
    return (inputs_x, b_rows, c_rows, x_scaled)

def span_states(activated, step_size, log_decay, resets, n_heads, head_size, n_state):
    inputs_x, b_rows, c_rows, x_scaled = split_inputs(activated, step_size, n_heads, head_size, n_state)
    cum_decay = jnp.cumsum(log_decay, axis=1)
    segment = jnp.cumsum(resets, axis=1)
    alive = (segment == segment[:, -1:]).astype(jnp.float32)
    weights = jnp.exp(cum_decay[:, -1:, :] - cum_decay) * alive[:, :, None]
    x_weighted = (x_scaled.astype(jnp.float32) * weights[..., None]).astype(jnp.bfloat16)
    states = contract('cshp,csn->chpn', x_weighted, b_rows)
    decays = jnp.exp(cum_decay[:, -1, :]) * (segment[:, -1:] == 0).astype(jnp.float32)
    return (decays, states)

def entry_weights(activated, cum_decay, segment, n_state, inner_width):
    c_rows = activated[..., inner_width + n_state:]
    entry = jnp.exp(cum_decay) * (segment == 0).astype(jnp.float32)[..., None]
    return (c_rows.astype(jnp.float32)[:, :, None, :] * entry[..., None]).astype(jnp.bfloat16)

def carried_terms(c_decayed, starts):
    return contract('cthn,chpn->cthp', c_decayed, starts.astype(jnp.bfloat16))

def span_outputs(activated, step_size, log_decay, resets, starts, skip_gain, n_heads, head_size, n_state):
    inputs_x, b_rows, c_rows, x_scaled = split_inputs(activated, step_size, n_heads, head_size, n_state)
    cum_decay = jnp.cumsum(log_decay, axis=1)
    segment = jnp.cumsum(resets, axis=1)
    span_len = activated.shape[1]
    scores = contract('ctn,csn->cts', c_rows, b_rows)
    position = jnp.arange(span_len)
    causal = position[:, None] >= position[None, :]
    allowed = causal[None] & (segment[:, :, None] == segment[:, None, :])
    cum_heads = jnp.swapaxes(cum_decay, 1, 2)
    exponent = cum_heads[:, :, :, None] - cum_heads[:, :, None, :]
    mask_heads = allowed[:, None]
    decay_matrix = jnp.where(mask_heads, jnp.exp(jnp.where(mask_heads, exponent, 0.0)), 0.0)
    mixing = (scores[:, None] * decay_matrix).astype(jnp.bfloat16)
    within = contract('chts,cshp->cthp', mixing, x_scaled)
    c_decayed = entry_weights(activated, cum_decay, segment, n_state, n_heads * head_size)
    summed = within + carried_terms(c_decayed, starts) + skip_gain[None, None, :, None] * inputs_x.astype(jnp.float32)
    return summed.astype(jnp.bfloat16)

def forward_sequence(row_data, step_raw, resets, conv_weight, conv_bias, dt_bias, decay_rate, skip_gain):
    length = row_data.shape[0]
    keep_rows = (1 - resets).astype(jnp.float32)
    prior_rows = jnp.zeros((K - 1, CH), jnp.float32)
    prior_keep = jnp.zeros((K - 1,), jnp.float32)
    activated = conv_silu(row_data, prior_rows, prior_keep, keep_rows, conv_weight, conv_bias)
    step_size, log_decay = step_sizes(step_raw, dt_bias, decay_rate)
    number = length // Q
    pieces = (activated.reshape(number, 1, Q, CH), step_size.reshape(number, 1, Q, H), log_decay.reshape(number, 1, Q, H), resets.reshape(number, 1, Q))

    def span_step(carried, piece):
        span_act, span_size, span_log, span_reset = piece
        decays, states = span_states(span_act, span_size, span_log, span_reset, H, P_SIZE, N)
        result = span_outputs(span_act, span_size, span_log, span_reset, carried[None], skip_gain, H, P_SIZE, N)
        return (decays[0][:, None, None] * carried + states[0], result[0])
    final_state, results = lax.scan(jax.checkpoint(span_step), jnp.zeros((H, P_SIZE, N), jnp.float32), pieces)
    return results.reshape(length, H * P_SIZE)

def reference(conv_input, dt_raw, packing, resets, conv_weight, conv_bias, dt_bias, decay_rate, skip_gain, grad_out):
    shard = (jnp.arange(SEQ_BLOCKS) // RB).astype(jnp.int32)
    target = (packing[:, :, 0] * SEQ_BLOCKS + shard[None, :] * RB + packing[:, :, 1]).reshape(-1).astype(jnp.int32)
    blocks = conv_input.astype(jnp.float32).reshape(SEQS * SEQ_BLOCKS, BLK, CH)
    packed = jnp.zeros_like(blocks).at[target].set(blocks).reshape(SEQS, SEQ_LEN, CH)
    step_blocks = dt_raw.astype(jnp.float32).reshape(SEQS * SEQ_BLOCKS, BLK, H)
    packed_dt = jnp.zeros_like(step_blocks).at[target].set(step_blocks).reshape(SEQS, SEQ_LEN, H)

    def one_sequence(piece):
        row_data, step_raw, flags_here, cotangent = piece

        def forward(rows_f, steps_f, weight, bias, step_bias, rate, gain):
            return forward_sequence(rows_f, steps_f, flags_here, weight, bias, step_bias, rate, gain)
        result, pullback = jax.vjp(forward, row_data, step_raw, conv_weight, conv_bias, dt_bias, decay_rate, skip_gain)
        return (result,) + tuple(pullback(cotangent))
    outputs = lax.map(one_sequence, (packed, packed_dt, resets, grad_out))
    layer_out, grad_rows, grad_steps, grad_weight, grad_bias, grad_step_bias, grad_rate, grad_gain = outputs
    grad_input = grad_rows.reshape(SEQS * SEQ_BLOCKS, BLK, CH)[target].reshape(SEQS, SEQ_LEN, CH).astype(jnp.bfloat16)
    grad_dt = grad_steps.reshape(SEQS * SEQ_BLOCKS, BLK, H)[target].reshape(SEQS, SEQ_LEN, H).astype(jnp.bfloat16)
    return (layer_out, grad_input, grad_dt, lax.optimization_barrier(jnp.sum(grad_weight, axis=0)), lax.optimization_barrier(jnp.sum(grad_bias, axis=0)), lax.optimization_barrier(jnp.sum(grad_step_bias, axis=0)), lax.optimization_barrier(jnp.sum(grad_rate, axis=0)), lax.optimization_barrier(jnp.sum(grad_gain, axis=0)))
```

```python
import functools

import jax
import jax.numpy as jnp
from jax import lax
from jax.experimental import pallas as pl
from jax.experimental.pallas import tpu as pltpu
from jax.sharding import PartitionSpec as P

F32 = jnp.float32
BF16 = jnp.bfloat16
LANES = 128
PAD = 8
WIDE = 256
LAG = 2
VMEM_LIMIT = 56 * 1024 * 1024
HIGH = lax.Precision.HIGHEST


def vmem():
    return pl.BlockSpec(memory_space=pltpu.VMEM)


def smem():
    return pl.BlockSpec(memory_space=pltpu.SMEM)


def dot(a, b, dims=((1,), (0,)), precision=None):
    return lax.dot_general(
        a, b, (dims, ((), ())), preferred_element_type=F32, precision=precision
    )


def iota(shape, dim):
    return lax.broadcasted_iota(jnp.int32, shape, dim)


def arrange_kernel(pack_ref, rows_ref, dt_ref, send_ref, tail_ref, tag_ref):
    held, block, width = send_ref.shape
    channels = rows_ref.shape[2]
    heads = dt_ref.shape[2]
    for j in range(held):
        to = pack_ref[j, 0]
        send_ref[to, :, :channels] = rows_ref[j]
        send_ref[to, :, channels:] = jnp.zeros((block, width - channels), BF16)
        send_ref[to, :, channels : channels + heads] = dt_ref[j]
        tail_ref[to] = rows_ref[j, block - 2 * PAD :, :].astype(F32)[PAD:].astype(BF16)
        tag_ref[to] = jnp.full((8, LANES), pack_ref[j, 1], jnp.int32)


def peers_barrier(seq_axis_peers, groups, me_s, me_d, n_seq):
    barrier = pltpu.get_barrier_semaphore()

    def tell(s, d):
        pl.semaphore_signal(
            barrier, inc=1, device_id={"seq": s, "dp": d}, device_id_type=pl.DeviceIdType.MESH
        )

    for k in range(1, groups):
        tell(me_s, lax.rem(me_d + k, groups))
    for step in (1, -1):
        ok = (me_s + step >= 0) & (me_s + step < n_seq)

        @pl.when(ok)
        def _():
            for d in range(groups if seq_axis_peers == "all" else 0):
                tell(me_s + step, d)

    pl.semaphore_wait(barrier, groups - 1 + groups * sides(me_s, n_seq))


def sides(me, count):
    return (me > 0).astype(jnp.int32) + (me < count - 1).astype(jnp.int32)


def remote(src, dst, ssem, rsem, s, d):
    return pltpu.make_async_remote_copy(
        src_ref=src,
        dst_ref=dst,
        send_sem=ssem,
        recv_sem=rsem,
        device_id={"seq": s, "dp": d},
        device_id_type=pl.DeviceIdType.MESH,
    )


def spread_kernel(
    n_seq, groups,
    send_ref, tail_ref, tag_ref, reset_ref,
    got_ref, gtag_ref, ptail_ref, ptag_ref, preset_ref,
    ss, rs, tss, trs, qss, qrs, uss, urs, wss, wrs, lsem,
):
    me_s, me_d = lax.axis_index("seq"), lax.axis_index("dp")
    peers_barrier("all", groups, me_s, me_d, n_seq)
    row_copies = []
    for k in range(1, groups):
        d = lax.rem(me_d + k, groups)
        a = remote(send_ref.at[d], got_ref.at[me_d], ss.at[k], rs.at[k], me_s, d)
        b = remote(tag_ref.at[d], gtag_ref.at[me_d], tss.at[k], trs.at[k], me_s, d)
        a.start()
        b.start()
        row_copies += [a, b]
    own = [
        pltpu.make_async_copy(send_ref.at[me_d], got_ref.at[me_d], lsem.at[0]),
        pltpu.make_async_copy(tag_ref.at[me_d], gtag_ref.at[me_d], lsem.at[1]),
    ]
    for c in own:
        c.start()

    def tails():
        out = []
        for k in range(groups):
            d = lax.rem(me_d + k, groups)
            out.append(remote(tail_ref.at[d], ptail_ref.at[me_d], qss.at[k], qrs.at[k], me_s + 1, d))
            out.append(remote(tag_ref.at[d], ptag_ref.at[me_d], uss.at[k], urs.at[k], me_s + 1, d))
        out.append(remote(reset_ref, preset_ref, wss, wrs, me_s + 1, me_d))
        return out

    @pl.when(me_s + 1 < n_seq)
    def _():
        for c in tails():
            c.start()

    @pl.when(me_s == 0)
    def _():
        ptail_ref[...] = jnp.zeros(ptail_ref.shape, BF16)
        ptag_ref[...] = jnp.zeros(ptag_ref.shape, jnp.int32)
        preset_ref[...] = jnp.zeros(preset_ref.shape, jnp.int32)

    for c in own:
        c.wait()
    for c in row_copies:
        c.wait()

    @pl.when(me_s + 1 < n_seq)
    def _():
        for c in tails():
            c.wait_send()

    @pl.when(me_s > 0)
    def _():
        for c in tails():
            c.wait_recv()


def token_values(dtp, bias_row, rate_row, reset_row):
    length = dtp.shape[0]
    t_i = iota((length, length), 0)
    s_i = iota((length, length), 1)
    raw = dtp + bias_row
    size = jnp.maximum(raw, 0.0) + jnp.log1p(jnp.exp(-jnp.abs(raw)))
    log_decay = -size * rate_row
    lower = (t_i >= s_i).astype(F32)
    cum = dot(lower, log_decay, precision=HIGH)
    cum_t = dot(log_decay, lower, ((0,), (1,)), precision=HIGH)
    flags = jnp.broadcast_to(reset_row.astype(F32), (length, length))
    seg_col = jnp.sum(jnp.where(t_i >= s_i, flags, 0.0), axis=1, keepdims=True)
    reset_col = jnp.sum(jnp.where(t_i == s_i, flags, 0.0), axis=1, keepdims=True)
    seg_row = jnp.sum(
        jnp.where(t_i <= s_i, jnp.broadcast_to(reset_col, (length, length)), 0.0),
        axis=0, keepdims=True,
    )
    last = cum[length - 1 : length, :]
    seg_last = seg_col[length - 1 : length, :]
    weight = jnp.where(seg_col == seg_last, jnp.exp(last - cum), 0.0)
    entry = jnp.where(seg_col == 0.0, jnp.exp(cum), 0.0)
    decay = jnp.where(seg_last == 0.0, jnp.exp(last), 0.0)
    allowed = (t_i >= s_i) & (seg_col == seg_row)
    return raw, size, cum, cum_t, weight, entry, decay, allowed, reset_col


def pair(x, i, head_size, rows):
    per = LANES // head_size
    lane = iota((rows, LANES), 1) // head_size
    out = jnp.broadcast_to(x[:, per * i : per * i + 1], (rows, LANES))
    for k in range(1, per):
        out = jnp.where(lane == k, x[:, per * i + k : per * i + k + 1], out)
    return out


def front_kernel(
    inner, head_size, n_state,
    tag_ref, ptag_ref,
    got_ref, ptail_ref, reset_ref, preset_ref, weight_ref, cbias_ref, sbias_ref, rate_ref, gout_ref,
    ext_ref, act_ref, slope_ref, dtp_ref, join_ref, state_ref, gstate_ref, decay_ref,
):
    groups, block, width = got_ref.shape
    length = act_ref.shape[0]
    channels = act_ref.shape[1]
    held = length // block
    for g in range(groups):
        slot = tag_ref[g, 0, 0] - 0
        start = pl.multiple_of(slot * block, block)
        ext_ref[pl.ds(start + PAD, block), :] = got_ref[g, :, :channels].astype(F32)
        dtp_ref[pl.ds(start, block), :] = got_ref[g, :, channels:].astype(F32)
    prior = jnp.zeros((PAD, channels), F32)
    for g in range(groups):
        prior = jnp.where(ptag_ref[g, 0, 0] == held - 1, ptail_ref[g].astype(F32), prior)
    ext_ref[0:PAD, :] = prior

    raw, size, cum, cum_t, wgt, ent, dec, allowed, reset_col = token_values(
        dtp_ref[...], sbias_ref[...], rate_ref[...], reset_ref[...]
    )
    prev = jnp.broadcast_to(preset_ref[...].astype(F32), (PAD, length))
    pick = iota((PAD, length), 1) == iota((PAD, length), 0) + (length - PAD)
    prev_col = jnp.sum(jnp.where(pick, prev, 0.0), axis=1, keepdims=True)
    flags = jnp.concatenate([prev_col, reset_col], axis=0)
    flags = jnp.broadcast_to(flags, (length + PAD, LANES))
    keep = 1.0 - flags
    j1 = keep[PAD:]
    j2 = j1 * keep[PAD - 1 : PAD - 1 + length]
    j3 = j2 * keep[PAD - 2 : PAD - 2 + length]
    join_ref[0] = j1
    join_ref[1] = j2
    join_ref[2] = j3
    for lo in range(0, channels, LANES):
        sl = slice(lo, lo + LANES)
        v = cbias_ref[:, sl] + weight_ref[3:4, sl] * ext_ref[PAD:, sl]
        v = v + weight_ref[2:3, sl] * (ext_ref[PAD - 1 : PAD - 1 + length, sl] * j1)
        v = v + weight_ref[1:2, sl] * (ext_ref[PAD - 2 : PAD - 2 + length, sl] * j2)
        v = v + weight_ref[0:1, sl] * (ext_ref[PAD - 3 : PAD - 3 + length, sl] * j3)
        sig = jax.nn.sigmoid(v)
        act_ref[:, sl] = (v * sig).astype(BF16)
        slope_ref[:, sl] = sig * (1.0 + v * (1.0 - sig))
    b_rows = act_ref[:, inner : inner + n_state]
    c_rows = act_ref[:, inner + n_state :]
    for i in range(inner // LANES):
        sl = slice(i * LANES, (i + 1) * LANES)
        at, lo = divmod(i * LANES, WIDE)
        xs = (act_ref[:, sl].astype(F32) * pair(size, i, head_size, length)).astype(BF16)
        xw = (xs.astype(F32) * pair(wgt, i, head_size, length)).astype(BF16)
        ed = (gout_ref[:, sl].astype(F32) * pair(ent, i, head_size, length)).astype(BF16)
        state_ref[at, :, lo : lo + LANES] = dot(b_rows, xw, ((0,), (0,))).astype(BF16)
        gstate_ref[at, :, lo : lo + LANES] = dot(c_rows, ed, ((0,), (0,))).astype(BF16)
        decay_ref[at, :, lo : lo + LANES] = pair(jnp.broadcast_to(dec, (8, LANES)), i, head_size, 8)


def chain_kernel(
    n_seq, state_ref, gstate_ref, decay_ref, enter_ref, after_ref,
    fout, bout, fin, bin_, fss, frs, bss, brs,
):
    me, me_d = lax.axis_index("seq"), lax.axis_index("dp")
    pieces = state_ref.shape[0]
    barrier = pltpu.get_barrier_semaphore()
    for step in (1, -1):
        ok = (me + step >= 0) & (me + step < n_seq)

        @pl.when(ok)
        def _():
            pl.semaphore_signal(
                barrier, inc=1, device_id={"seq": me + step, "dp": me_d},
                device_id_type=pl.DeviceIdType.MESH,
            )

    pl.semaphore_wait(barrier, sides(me, n_seq))

    def one(c, first, final, local, got, out, result, ssem, rsem, to):
        copy = remote(out.at[c], got.at[c], ssem.at[c], rsem.at[c], to, me_d)

        @pl.when(first)
        def _():
            got[c] = jnp.zeros(got.shape[1:], BF16)

        @pl.when(jnp.logical_not(first))
        def _():
            copy.wait_recv()

        result[c] = got[c]

        @pl.when(jnp.logical_not(final))
        def _():
            out[c] = (decay_ref[c, 0:1, :] * got[c].astype(F32) + local[c].astype(F32)).astype(BF16)
            copy.start()

    def body(v, carry):
        cf = v - LAG * me
        cb = v - LAG * (n_seq - 1 - me)

        @pl.when((cf >= 0) & (cf < pieces))
        def _():
            one(cf, me == 0, me == n_seq - 1, state_ref, fin, fout, enter_ref, fss, frs, me + 1)

        @pl.when((cb >= 0) & (cb < pieces))
        def _():
            one(cb, me == n_seq - 1, me == 0, gstate_ref, bin_, bout, after_ref, bss, brs, me - 1)

        return carry

    lax.fori_loop(0, LAG * (n_seq - 1) + pieces, body, 0)

    def drain(c, carry):
        @pl.when(me < n_seq - 1)
        def _():
            remote(fout.at[c], fin.at[c], fss.at[c], frs.at[c], me + 1, me_d).wait_send()

        @pl.when(me > 0)
        def _():
            remote(bout.at[c], bin_.at[c], bss.at[c], brs.at[c], me - 1, me_d).wait_send()

        return carry

    lax.fori_loop(0, pieces, drain, 0)


def split_dot(a, b, dims=((1,), (0,))):
    hi = a.astype(BF16)
    lo = (a - hi.astype(F32)).astype(BF16)
    return dot(hi, b, dims) + dot(lo, b, dims)


def back_kernel(
    inner, head_size, n_state, heads, share,
    tag_ref,
    ext_ref, act_ref, slope_ref, dtp_ref, join_ref, enter_ref, after_ref,
    reset_ref, weight_ref, sbias_ref, rate_ref, gain_ref, gout_ref,
    out_ref, back_ref, spill_ref, param_ref,
    dv_ref, p_ref, grad_ref, gdt_ref, dcum_ref, dsize_ref, tot_ref,
):
    length, channels = act_ref.shape
    groups, block, _ = back_ref.shape
    per = LANES // head_size
    raw, size, cum, cum_t, wgt, ent, dec, allowed, _ = token_values(
        dtp_ref[...], sbias_ref[...], rate_ref[...], reset_ref[...]
    )
    gain = gain_ref[...]
    b_rows = act_ref[:, inner : inner + n_state]
    c_rows = act_ref[:, inner + n_state :]
    scores = dot(c_rows, b_rows, ((1,), (1,)))
    dcum_ref[...] = jnp.zeros((length, LANES), F32)
    dsize_ref[...] = jnp.zeros((length, LANES), F32)
    tot_ref[...] = jnp.zeros((16, LANES), F32)
    dscore = jnp.zeros((length, length), F32)
    db = jnp.zeros((length, n_state), F32)
    dc = jnp.zeros((length, n_state), F32)
    lane = iota((length, LANES), 1) // head_size
    row_head = iota((LANES, LANES), 0) // head_size
    col_head = iota((LANES, LANES), 1)
    dec8 = jnp.broadcast_to(dec, (8, LANES))
    gain8 = jnp.broadcast_to(gain, (8, LANES))
    for i in range(inner // LANES):
        sl = slice(i * LANES, (i + 1) * LANES)
        at, lo = divmod(i * LANES, WIDE)
        enter = enter_ref[at, :, lo : lo + LANES]
        after = after_ref[at, :, lo : lo + LANES]
        x = act_ref[:, sl].astype(F32)
        do = gout_ref[:, sl]
        do32 = do.astype(F32)
        size_b = pair(size, i, head_size, length)
        wgt_b = pair(wgt, i, head_size, length)
        ent_b = pair(ent, i, head_size, length)
        gain_b = pair(gain8, i, head_size, 8)[0:1]
        dec_b = pair(dec8, i, head_size, 8)[0:1]
        xs = (x * size_b).astype(BF16)
        xs32 = xs.astype(F32)
        within = jnp.zeros((length, LANES), F32)
        dxs = jnp.zeros((length, LANES), F32)
        for k in range(per):
            h = per * i + k
            expo = cum[:, h : h + 1] - cum_t[h : h + 1, :]
            decay = jnp.exp(jnp.where(allowed, expo, -1e30))
            mixing = (scores * decay).astype(BF16)
            mine = lane == k
            within = jnp.where(mine, dot(mixing, xs), within)
            dxs = jnp.where(mine, dot(mixing, do, ((0,), (0,))), dxs)
            dmix = dot(jnp.where(mine, do32, 0.0).astype(BF16), xs, ((1,), (1,)))
            dscore = dscore + dmix * decay
        y = within + ent_b * dot(c_rows, enter)
        out_ref[:, sl] = (y + gain_b * x).astype(BF16)
        ba = wgt_b * dot(b_rows, after)
        dxs = dxs + ba
        dv_ref[:, sl] = (dxs * size_b + gain_b * do32) * slope_ref[:, sl]
        xw = (xs32 * wgt_b).astype(BF16)
        ed = (do32 * ent_b).astype(BF16)
        db = db + dot(xw, after, ((1,), (1,)))
        dc = dc + dot(ed, enter, ((1,), (1,)))
        ind = (row_head + per * i == col_head).astype(BF16)
        dcum_ref[...] += split_dot(do32 * y - xs32 * dxs, ind)
        dsize_ref[...] += split_dot(dxs * x, ind)
        t3 = jnp.sum(xs32 * ba, axis=0, keepdims=True) + dec_b * jnp.sum(
            after.astype(F32) * enter.astype(F32), axis=0, keepdims=True
        )
        t5 = jnp.sum(do32 * x, axis=0, keepdims=True)
        both = jnp.concatenate(
            [jnp.broadcast_to(t3, (8, LANES)), jnp.broadcast_to(t5, (8, LANES))], axis=0
        )
        tot_ref[...] += split_dot(both, ind)
    dscore = dscore.astype(BF16)
    dc = dc + dot(dscore, b_rows)
    db = db + dot(dscore, c_rows, ((0,), (0,)))
    slb = slice(inner, inner + n_state)
    slc = slice(inner + n_state, channels)
    dv_ref[:, slb] = db * slope_ref[:, slb]
    dv_ref[:, slc] = dc * slope_ref[:, slc]

    t_i = iota((length, length), 0)
    s_i = iota((length, length), 1)
    is_last = iota((length, LANES), 0) == length - 1
    dcum = dcum_ref[...] + jnp.where(is_last, tot_ref[0:1, :], 0.0)
    dlog = dot((s_i >= t_i).astype(F32), dcum, precision=HIGH)
    dsize = dsize_ref[...] - dlog * rate_ref[...]
    draw = dsize * jax.nn.sigmoid(raw)
    gdt_ref[...] = draw
    param_ref[...] = jnp.zeros(param_ref.shape, F32)
    param_ref[0, 5:6, 0:LANES] = jnp.sum(draw, axis=0, keepdims=True)
    param_ref[0, 6:7, 0:LANES] = -jnp.sum(dlog * size, axis=0, keepdims=True)
    param_ref[0, 7:8, 0:LANES] = tot_ref[8:9, :]

    p_ref[:, 0:PAD, :] = jnp.zeros((3, PAD, LANES), F32)
    p_ref[:, PAD + length :, :] = jnp.zeros((3, PAD, LANES), F32)
    zeros = jnp.zeros((PAD, LANES), F32)
    for lo in range(0, channels, LANES):
        sl = slice(lo, lo + LANES)
        at, off = divmod(lo, share)
        col = slice(off, off + LANES)
        dv = dv_ref[:, sl]
        total = jnp.concatenate([zeros, weight_ref[3:4, sl] * dv], axis=0)
        param_ref[at, 3:4, col] = jnp.sum(dv * ext_ref[PAD:, sl], axis=0, keepdims=True)
        param_ref[at, 4:5, col] = jnp.sum(dv, axis=0, keepdims=True)
        for k in range(1, 4):
            pk = dv * join_ref[k - 1]
            p_ref[k - 1, PAD : PAD + length, :] = pk
            param_ref[at, 3 - k : 4 - k, col] = jnp.sum(
                pk * ext_ref[PAD - k : PAD - k + length, sl], axis=0, keepdims=True
            )
            total = total + weight_ref[3 - k : 4 - k, sl] * p_ref[k - 1, k : k + length + PAD, :]
        spill_ref[:, sl] = total[0:PAD].astype(BF16)
        grad_ref[:, sl] = total[PAD:]
    for g in range(groups):
        start = pl.multiple_of(tag_ref[g, 0, 0] * block, block)
        back_ref[g, :, :channels] = grad_ref[pl.ds(start, block), :].astype(BF16)
        back_ref[g, :, channels:] = gdt_ref[pl.ds(start, block), :].astype(BF16)


def return_kernel(
    n_seq, groups,
    back_ref, spill_ref, param_ref,
    ret_ref, rspill_ref, total_ref,
    part, mid, fin,
    ss, rs, qss, qrs, ass, ars, bss, brs, css, crs, lsem,
):
    me_s, me_d = lax.axis_index("seq"), lax.axis_index("dp")
    barrier = pltpu.get_barrier_semaphore()

    def tell(s, d):
        pl.semaphore_signal(
            barrier, inc=1, device_id={"seq": s, "dp": d}, device_id_type=pl.DeviceIdType.MESH
        )

    for k in range(1, groups):
        tell(me_s, lax.rem(me_d + k, groups))
    for k in range(1, n_seq):
        tell(lax.rem(me_s + k, n_seq), me_d)
    for step in (1, -1):
        ok = (me_s + step >= 0) & (me_s + step < n_seq)

        @pl.when(ok)
        def _():
            for k in range(1, groups):
                tell(me_s + step, lax.rem(me_d + k, groups))

    pl.semaphore_wait(barrier, groups + n_seq - 2 + (groups - 1) * sides(me_s, n_seq))

    scatter = []
    for k in range(1, n_seq):
        s = lax.rem(me_s + k, n_seq)
        scatter.append(remote(param_ref.at[s], part.at[k], ass.at[k], ars.at[k], s, me_d))
    for c in scatter:
        c.start()
    rows = []
    for k in range(1, groups):
        d = lax.rem(me_d + k, groups)
        rows.append(remote(back_ref.at[d], ret_ref.at[me_d], ss.at[k], rs.at[k], me_s, d))
    for c in rows:
        c.start()
    own = pltpu.make_async_copy(back_ref.at[me_d], ret_ref.at[me_d], lsem)
    own.start()

    def spills():
        return [
            remote(
                spill_ref, rspill_ref.at[me_d], qss.at[k], qrs.at[k], me_s - 1,
                lax.rem(me_d + k, groups),
            )
            for k in range(groups)
        ]

    @pl.when(me_s > 0)
    def _():
        for c in spills():
            c.start()

    @pl.when(me_s == n_seq - 1)
    def _():
        rspill_ref[...] = jnp.zeros(rspill_ref.shape, BF16)

    for c in scatter:
        c.wait()
    mine = param_ref[me_s]
    for k in range(1, n_seq):
        mine = mine + part[k]
    mid[0] = mine
    across = [
        remote(mid.at[0], mid.at[k], bss.at[k], brs.at[k], me_s, lax.rem(me_d + k, groups))
        for k in range(1, groups)
    ]
    for c in across:
        c.start()
    for c in across:
        c.wait()
    total = jnp.zeros(mine.shape, F32)
    for d in range(groups):
        total = total + mid[lax.rem(me_d - d + groups, groups)]
    fin[...] = total
    total_ref[me_s] = total
    gather = [
        remote(fin, total_ref.at[me_s], css.at[k], crs.at[k], lax.rem(me_s + k, n_seq), me_d)
        for k in range(1, n_seq)
    ]
    for c in gather:
        c.start()
    for c in rows:
        c.wait()
    own.wait()

    @pl.when(me_s > 0)
    def _():
        for c in spills():
            c.wait_send()

    @pl.when(me_s < n_seq - 1)
    def _():
        for c in spills():
            c.wait_recv()

    for c in gather:
        c.wait()


def place_kernel(
    share, pack_ref, ret_ref, rspill_ref, total_ref,
    gin_ref, gdt_ref, gw_ref, gb_ref, gsb_ref, grate_ref, ggain_ref,
):
    held, block, channels = gin_ref.shape
    heads = gdt_ref.shape[2]
    for j in range(held):
        g = pack_ref[j, 0]
        gin_ref[j] = ret_ref[g, :, :channels]
        gdt_ref[j] = ret_ref[g, :, channels : channels + heads]
        low = ret_ref[g, block - 2 * PAD :, :channels].astype(F32)
        extra = rspill_ref[g].astype(F32)
        last = pack_ref[j, 1] == held - 1
        extra = jnp.where(last, extra, 0.0)
        gin_ref[j, block - 2 * PAD :, :] = jnp.concatenate(
            [low[:PAD], low[PAD:] + extra], axis=0
        ).astype(BF16)
    for lo in range(0, channels, LANES):
        at, off = divmod(lo, share)
        gw_ref[:, lo : lo + LANES] = total_ref[at, 0:4, off : off + LANES]
        gb_ref[:, lo : lo + LANES] = total_ref[at, 4:5, off : off + LANES]
    gsb_ref[...] = total_ref[0, 5:6, 0:heads]
    grate_ref[...] = total_ref[0, 6:7, 0:heads]
    ggain_ref[...] = total_ref[0, 7:8, 0:heads]


def shape(dims, kind):
    return jax.ShapeDtypeStruct(dims, kind)


def call(kernel, ins, outs, scratch=(), cid=None):
    extra = {} if cid is None else {"collective_id": cid, "has_side_effects": True}
    return pl.pallas_call(
        kernel,
        out_shape=outs,
        in_specs=ins,
        out_specs=tuple(vmem() for _ in outs),
        scratch_shapes=list(scratch),
        compiler_params=pltpu.CompilerParams(vmem_limit_bytes=VMEM_LIMIT, **extra),
    )


def per_device(
    conv_input, dt_raw, packing, resets, conv_weight, conv_bias, dt_bias, decay_rate, skip_gain, grad_out
):
    groups = lax.axis_size("dp")
    n_seq = lax.axis_size("seq")
    length, channels = conv_input.shape[1:]
    heads = dt_raw.shape[2]
    inner = grad_out.shape[2]
    head_size = inner // heads
    n_state = (channels - inner) // 2
    held = packing.shape[1]
    block = length // held
    width = channels + LANES
    pack = packing[0]
    dma = pltpu.SemaphoreType.DMA
    row = lambda a: a.reshape(1, -1)
    padded = lambda a: jnp.pad(row(a), ((0, 0), (0, LANES - heads)))

    send, tail, tag = call(
        arrange_kernel,
        [smem(), vmem(), vmem()],
        (
            shape((groups, block, width), BF16),
            shape((groups, PAD, channels), BF16),
            shape((groups, 8, LANES), jnp.int32),
        ),
    )(pack, conv_input[0].reshape(held, block, channels), dt_raw[0].reshape(held, block, heads))

    got, gtag, ptail, ptag, preset = call(
        functools.partial(spread_kernel, n_seq, groups),
        [vmem()] * 4,
        (
            shape((groups, block, width), BF16),
            shape((groups, 8, LANES), jnp.int32),
            shape((groups, PAD, channels), BF16),
            shape((groups, 8, LANES), jnp.int32),
            shape((1, length), jnp.int32),
        ),
        [dma((groups,))] * 8 + [dma, dma, dma((2,))],
        cid=0,
    )(send, tail, tag, resets)

    sbias, rate, gain = padded(dt_bias), padded(decay_rate), padded(skip_gain)
    pieces = inner // WIDE
    state_shape = shape((pieces, n_state, WIDE), BF16)
    ext, act, slope, dtp, join, state, gstate, decay = call(
        functools.partial(front_kernel, inner, head_size, n_state),
        [smem(), smem()] + [vmem()] * 9,
        (
            shape((length + PAD, channels), F32),
            shape((length, channels), BF16),
            shape((length, channels), F32),
            shape((length, LANES), F32),
            shape((3, length, LANES), F32),
            state_shape,
            state_shape,
            shape((pieces, 8, WIDE), F32),
        ),
    )(
        gtag[:, :1, :1], ptag[:, :1, :1], got, ptail, resets, preset, conv_weight, row(conv_bias),
        sbias, rate, grad_out[0],
    )

    enter, after = call(
        functools.partial(chain_kernel, n_seq),
        [vmem()] * 3,
        (state_shape, state_shape),
        [pltpu.VMEM(state_shape.shape, BF16)] * 4 + [dma((pieces,))] * 4,
        cid=1,
    )(state, gstate, decay)

    tiles = channels // LANES
    share = -(-tiles // n_seq) * LANES
    params = shape((n_seq, 8, share), F32)
    out, back, spill, param = call(
        functools.partial(back_kernel, inner, head_size, n_state, heads, share),
        [smem()] + [vmem()] * 13,
        (
            shape((length, inner), BF16),
            shape((groups, block, width), BF16),
            shape((PAD, channels), BF16),
            params,
        ),
        [
            pltpu.VMEM((length, channels), F32),
            pltpu.VMEM((3, length + 2 * PAD, LANES), F32),
            pltpu.VMEM((length, channels), F32),
            pltpu.VMEM((length, LANES), F32),
            pltpu.VMEM((length, LANES), F32),
            pltpu.VMEM((length, LANES), F32),
            pltpu.VMEM((16, LANES), F32),
        ],
    )(
        gtag[:, :1, :1], ext, act, slope, dtp, join, enter, after, resets, conv_weight, sbias, rate,
        gain, grad_out[0],
    )

    ret, rspill, total = call(
        functools.partial(return_kernel, n_seq, groups),
        [vmem()] * 3,
        (
            shape((groups, block, width), BF16),
            shape((groups, PAD, channels), BF16),
            params,
        ),
        [
            pltpu.VMEM((n_seq, 8, share), F32),
            pltpu.VMEM((groups, 8, share), F32),
            pltpu.VMEM((8, share), F32),
        ]
        + [dma((groups,))] * 4
        + [dma((n_seq,))] * 2
        + [dma((groups,))] * 2
        + [dma((n_seq,))] * 2
        + [dma],
        cid=2,
    )(back, spill, param)

    gin, gdt, gw, gb, gsb, grate, ggain = call(
        functools.partial(place_kernel, share),
        [smem()] + [vmem()] * 3,
        (
            shape((held, block, channels), BF16),
            shape((held, block, heads), BF16),
            shape((4, channels), F32),
            shape((1, channels), F32),
            shape((1, heads), F32),
            shape((1, heads), F32),
            shape((1, heads), F32),
        ),
    )(pack, ret, rspill, total)
    return (
        out[None],
        gin.reshape(1, length, channels),
        gdt.reshape(1, length, heads),
        gw,
        gb[0],
        gsb[0],
        grate[0],
        ggain[0],
    )


def solution(mesh):
    tokens = P("dp", "seq", None)
    in_specs = (tokens, tokens, tokens, P("dp", "seq"), P(), P(), P(), P(), P(), tokens)
    out_specs = (tokens, tokens, tokens, P(), P(), P(), P(), P())
    return jax.shard_map(
        per_device, mesh=mesh, in_specs=in_specs, out_specs=out_specs, check_vma=False
    )
```

```python
import functools

import jax
import jax.numpy as jnp
from jax import lax
from jax.experimental import pallas as pl
from jax.experimental.pallas import tpu as pltpu
from jax.sharding import PartitionSpec as P

F32 = jnp.float32
BF16 = jnp.bfloat16
LANES = 128
PAD = 8
WIDE = 256
LAG = 3
VMEM_LIMIT = 56 * 1024 * 1024
HIGH = lax.Precision.HIGHEST


def vmem():
    return pl.BlockSpec(memory_space=pltpu.VMEM)


def smem():
    return pl.BlockSpec(memory_space=pltpu.SMEM)


def dot(a, b, dims=((1,), (0,)), precision=None):
    return lax.dot_general(
        a, b, (dims, ((), ())), preferred_element_type=F32, precision=precision
    )


def iota(shape, dim):
    return lax.broadcasted_iota(jnp.int32, shape, dim)


def arrange_kernel(pack_ref, rows_ref, dt_ref, send_ref, tail_ref, tag_ref):
    held, block, width = send_ref.shape
    channels = rows_ref.shape[2]
    heads = dt_ref.shape[0]
    steps = jnp.transpose(dt_ref[...].astype(F32))
    for j in range(held):
        to = pack_ref[0, j]
        send_ref[to, :, :channels] = rows_ref[j]
        send_ref[to, :, channels:] = jnp.zeros((block, width - channels), BF16)
        send_ref[to, :, channels : channels + heads] = steps[j * block : (j + 1) * block].astype(BF16)
        tail_ref[to] = rows_ref[j, block - 2 * PAD :, :].astype(F32)[PAD:].astype(BF16)
        tag_ref[to] = jnp.full((8, LANES), pack_ref[1, j], jnp.int32)


def home(s, d, n_seq, groups):
    if (n_seq, groups) != (8, 4):
        return s, d
    sp, dp = lax.rem(s, 2), lax.rem(d, 2)
    return s - sp + dp, d - dp + sp


def tell(s, d):
    pl.semaphore_signal(
        pltpu.get_barrier_semaphore(), inc=1, device_id={"seq": s, "dp": d},
        device_id_type=pl.DeviceIdType.MESH,
    )


def one_if(cond):
    return jnp.where(cond, 1, 0).astype(jnp.int32)


def remote(src, dst, ssem, rsem, s, d):
    return pltpu.make_async_remote_copy(
        src_ref=src,
        dst_ref=dst,
        send_sem=ssem,
        recv_sem=rsem,
        device_id={"seq": s, "dp": d},
        device_id_type=pl.DeviceIdType.MESH,
    )


def spread_kernel(
    n_seq, groups,
    send_ref, tail_ref, tag_ref, reset_ref, gout_ref,
    got_ref, gtag_ref, ptail_ref, ptag_ref, preset_ref, oreset_ref, ogout_ref,
    ss, rs, tss, trs, qss, qrs, uss, urs, wss, wrs,
):
    me_s, me_d = lax.axis_index("seq"), lax.axis_index("dp")
    vs, vd = home(me_s, me_d, n_seq, groups)

    for j in range(groups):

        @pl.when((vs != me_s) | (j != me_d))
        def _():
            tell(vs, j)

        @pl.when((vs > 0) & ((vs - 1 != me_s) | (j != me_d)))
        def _():
            tell(vs - 1, j)

    after = me_s + 1 < n_seq
    count = groups - one_if(vs == me_s)
    count = count + jnp.where(after, groups - one_if(vs == me_s + 1), 0)
    pl.semaphore_wait(pltpu.get_barrier_semaphore(), count)

    def to_all(shard, pairs_of, act):
        for k in range(groups):
            g = lax.rem(me_d + k, groups)
            s, d = home(shard, g, n_seq, groups)
            mine = (s == me_s) & (d == me_d)
            pairs = pairs_of(g)

            @pl.when(mine)
            def _():
                for n, (src, dst, ssem, rsem) in enumerate(pairs):
                    act(pltpu.make_async_copy(src, dst, ssem), True)

            @pl.when(jnp.logical_not(mine))
            def _():
                for src, dst, ssem, rsem in pairs:
                    act(remote(src, dst, ssem, rsem, s, d), False)

    def heads_of(g):
        return [
            (tag_ref.at[g], gtag_ref.at[me_d], tss.at[g], trs.at[me_d]),
            (send_ref.at[g], got_ref.at[me_d], ss.at[g], rs.at[me_d]),
        ]

    def tails_of(g):
        return [
            (tag_ref.at[g], ptag_ref.at[me_d], uss.at[g], urs.at[me_d]),
            (tail_ref.at[g], ptail_ref.at[me_d], qss.at[g], qrs.at[me_d]),
        ]

    def own_values(act):
        s, d = vs, vd
        mine = (s == me_s) & (d == me_d)
        pairs = [
            (reset_ref, oreset_ref, wss.at[0], wrs.at[0]),
            (gout_ref, ogout_ref, wss.at[1], wrs.at[1]),
        ]

        @pl.when(mine)
        def _():
            for src, dst, ssem, rsem in pairs:
                act(pltpu.make_async_copy(src, dst, ssem), True)

        @pl.when(jnp.logical_not(mine))
        def _():
            for src, dst, ssem, rsem in pairs:
                act(remote(src, dst, ssem, rsem, s, d), False)

    def next_reset(act):
        s, d = home(me_s + 1, me_d, n_seq, groups)
        mine = (s == me_s) & (d == me_d)

        @pl.when(mine)
        def _():
            act(pltpu.make_async_copy(reset_ref, preset_ref, wss.at[2]), True)

        @pl.when(jnp.logical_not(mine))
        def _():
            act(remote(reset_ref, preset_ref, wss.at[2], wrs.at[2], s, d), False)

    start = lambda c, local: c.start()
    sent = lambda c, local: c.wait() if local else c.wait_send()
    to_all(me_s, heads_of, start)

    @pl.when(after)
    def _():
        to_all(me_s + 1, tails_of, start)
        next_reset(start)

    own_values(start)

    @pl.when(vs == 0)
    def _():
        ptail_ref[...] = jnp.zeros(ptail_ref.shape, BF16)
        ptag_ref[...] = jnp.zeros(ptag_ref.shape, jnp.int32)
        preset_ref[...] = jnp.zeros(preset_ref.shape, jnp.int32)

    for j in range(groups):

        @pl.when((vs != me_s) | (j != me_d))
        def _():
            remote(tag_ref.at[j], gtag_ref.at[j], tss.at[j], trs.at[j], vs, j).wait_recv()
            remote(send_ref.at[j], got_ref.at[j], ss.at[j], rs.at[j], vs, j).wait_recv()

        @pl.when((vs > 0) & ((vs - 1 != me_s) | (j != me_d)))
        def _():
            remote(tag_ref.at[j], ptag_ref.at[j], uss.at[j], urs.at[j], vs - 1, j).wait_recv()
            remote(tail_ref.at[j], ptail_ref.at[j], qss.at[j], qrs.at[j], vs - 1, j).wait_recv()

    @pl.when((vs != me_s) | (vd != me_d))
    def _():
        remote(reset_ref, oreset_ref, wss.at[0], wrs.at[0], vs, vd).wait_recv()
        remote(gout_ref, ogout_ref, wss.at[1], wrs.at[1], vs, vd).wait_recv()

    @pl.when((vs > 0) & ((vs - 1 != me_s) | (vd != me_d)))
    def _():
        remote(reset_ref, preset_ref, wss.at[2], wrs.at[2], vs - 1, vd).wait_recv()

    to_all(me_s, heads_of, sent)

    @pl.when(after)
    def _():
        to_all(me_s + 1, tails_of, sent)
        next_reset(sent)

    own_values(sent)


def token_values(dtp, bias_row, rate_row, reset_row):
    length = dtp.shape[0]
    t_i = iota((length, length), 0)
    s_i = iota((length, length), 1)
    raw = dtp + bias_row
    size = jnp.maximum(raw, 0.0) + jnp.log1p(jnp.exp(-jnp.abs(raw)))
    log_decay = -size * rate_row
    lower = (t_i >= s_i).astype(F32)
    cum = dot(lower, log_decay, precision=HIGH)
    cum_t = dot(log_decay, lower, ((0,), (1,)), precision=HIGH)
    flags = jnp.broadcast_to(reset_row.astype(F32), (length, length))
    seg_col = jnp.sum(jnp.where(t_i >= s_i, flags, 0.0), axis=1, keepdims=True)
    reset_col = jnp.sum(jnp.where(t_i == s_i, flags, 0.0), axis=1, keepdims=True)
    seg_row = jnp.sum(
        jnp.where(t_i <= s_i, jnp.broadcast_to(reset_col, (length, length)), 0.0),
        axis=0, keepdims=True,
    )
    last = cum[length - 1 : length, :]
    seg_last = seg_col[length - 1 : length, :]
    weight = jnp.where(seg_col == seg_last, jnp.exp(last - cum), 0.0)
    entry = jnp.where(seg_col == 0.0, jnp.exp(cum), 0.0)
    decay = jnp.where(seg_last == 0.0, jnp.exp(last), 0.0)
    allowed = (t_i >= s_i) & (seg_col == seg_row)
    return raw, size, cum, cum_t, weight, entry, decay, allowed, reset_col


def lane_row(ref):
    values = ref[...].reshape(1, -1)
    return jnp.concatenate([values, jnp.zeros((1, LANES - values.shape[1]), F32)], axis=1)


def pair(x, i, head_size, rows):
    per = LANES // head_size
    lane = iota((rows, LANES), 1) // head_size
    out = jnp.broadcast_to(x[:, per * i : per * i + 1], (rows, LANES))
    for k in range(1, per):
        out = jnp.where(lane == k, x[:, per * i + k : per * i + k + 1], out)
    return out


def front_kernel(
    inner, head_size, n_state,
    tag_ref, ptag_ref,
    got_ref, ptail_ref, reset_ref, preset_ref, weight_ref, cbias_ref, sbias_ref, rate_ref, gout_ref,
    ext_ref, act_ref, slope_ref, dtp_ref, join_ref, state_ref, gstate_ref, decay_ref,
):
    groups, block, width = got_ref.shape
    length = act_ref.shape[0]
    channels = act_ref.shape[1]
    held = length // block
    for g in range(groups):
        slot = tag_ref[g, 0, 0] - 0
        start = pl.multiple_of(slot * block, block)
        ext_ref[pl.ds(start + PAD, block), :] = got_ref[g, :, :channels].astype(F32)
        dtp_ref[pl.ds(start, block), :] = got_ref[g, :, channels:].astype(F32)
    prior = jnp.zeros((PAD, channels), F32)
    for g in range(groups):
        prior = jnp.where(ptag_ref[g, 0, 0] == held - 1, ptail_ref[g].astype(F32), prior)
    ext_ref[0:PAD, :] = prior

    rate = lane_row(rate_ref)
    raw, size, cum, cum_t, wgt, ent, dec, allowed, reset_col = token_values(
        dtp_ref[...], lane_row(sbias_ref), rate, reset_ref[...]
    )
    prev = jnp.broadcast_to(preset_ref[...].astype(F32), (PAD, length))
    pick = iota((PAD, length), 1) == iota((PAD, length), 0) + (length - PAD)
    prev_col = jnp.sum(jnp.where(pick, prev, 0.0), axis=1, keepdims=True)
    flags = jnp.concatenate([prev_col, reset_col], axis=0)
    flags = jnp.broadcast_to(flags, (length + PAD, LANES))
    keep = 1.0 - flags
    j1 = keep[PAD:]
    j2 = j1 * keep[PAD - 1 : PAD - 1 + length]
    j3 = j2 * keep[PAD - 2 : PAD - 2 + length]
    join_ref[0] = j1
    join_ref[1] = j2
    join_ref[2] = j3
    for lo in range(0, channels, LANES):
        sl = slice(lo, lo + LANES)
        v = cbias_ref[sl].reshape(1, LANES) + weight_ref[3:4, sl] * ext_ref[PAD:, sl]
        v = v + weight_ref[2:3, sl] * (ext_ref[PAD - 1 : PAD - 1 + length, sl] * j1)
        v = v + weight_ref[1:2, sl] * (ext_ref[PAD - 2 : PAD - 2 + length, sl] * j2)
        v = v + weight_ref[0:1, sl] * (ext_ref[PAD - 3 : PAD - 3 + length, sl] * j3)
        sig = jax.nn.sigmoid(v)
        act_ref[:, sl] = (v * sig).astype(BF16)
        slope_ref[:, sl] = sig * (1.0 + v * (1.0 - sig))
    b_rows = act_ref[:, inner : inner + n_state]
    c_rows = act_ref[:, inner + n_state :]
    for i in range(inner // LANES):
        sl = slice(i * LANES, (i + 1) * LANES)
        at, lo = divmod(i * LANES, WIDE)
        xs = (act_ref[:, sl].astype(F32) * pair(size, i, head_size, length)).astype(BF16)
        xw = (xs.astype(F32) * pair(wgt, i, head_size, length)).astype(BF16)
        ed = (gout_ref[:, sl].astype(F32) * pair(ent, i, head_size, length)).astype(BF16)
        state_ref[at, :, lo : lo + LANES] = dot(b_rows, xw, ((0,), (0,))).astype(BF16)
        gstate_ref[at, :, lo : lo + LANES] = dot(c_rows, ed, ((0,), (0,))).astype(BF16)
        decay_ref[at, :, lo : lo + LANES] = pair(jnp.broadcast_to(dec, (8, LANES)), i, head_size, 8)


def chain_kernel(
    n_seq, groups, state_ref, gstate_ref, decay_ref, enter_ref, after_ref,
    fout, bout, fin, bin_, fss, frs, bss, brs,
):
    me, seq = home(lax.axis_index("seq"), lax.axis_index("dp"), n_seq, groups)
    pieces = state_ref.shape[0]
    for step in (1, -1):

        @pl.when((me + step >= 0) & (me + step < n_seq))
        def _():
            tell(*home(me + step, seq, n_seq, groups))

    pl.semaphore_wait(
        pltpu.get_barrier_semaphore(), one_if(me > 0) + one_if(me < n_seq - 1)
    )

    def one(c, first, final, local, got, out, result, ssem, rsem, to):
        copy = remote(out.at[c], got.at[c], ssem.at[c], rsem.at[c], *home(to, seq, n_seq, groups))

        @pl.when(first)
        def _():
            got[c] = jnp.zeros(got.shape[1:], BF16)

        @pl.when(jnp.logical_not(first))
        def _():
            copy.wait_recv()

        result[c] = got[c]

        @pl.when(jnp.logical_not(final))
        def _():
            out[c] = (decay_ref[c, 0:1, :] * got[c].astype(F32) + local[c].astype(F32)).astype(BF16)
            copy.start()

    def body(v, carry):
        cf = v - LAG * me
        cb = v - LAG * (n_seq - 1 - me)

        @pl.when((cf >= 0) & (cf < pieces))
        def _():
            one(cf, me == 0, me == n_seq - 1, state_ref, fin, fout, enter_ref, fss, frs, me + 1)

        @pl.when((cb >= 0) & (cb < pieces))
        def _():
            one(cb, me == n_seq - 1, me == 0, gstate_ref, bin_, bout, after_ref, bss, brs, me - 1)

        return carry

    lax.fori_loop(0, LAG * (n_seq - 1) + pieces, body, 0)

    def drain(c, carry):
        @pl.when(me < n_seq - 1)
        def _():
            remote(fout.at[c], fin.at[c], fss.at[c], frs.at[c], *home(me + 1, seq, n_seq, groups)).wait_send()

        @pl.when(me > 0)
        def _():
            remote(bout.at[c], bin_.at[c], bss.at[c], brs.at[c], *home(me - 1, seq, n_seq, groups)).wait_send()

        return carry

    lax.fori_loop(0, pieces, drain, 0)


def split_dot(a, b, dims=((1,), (0,))):
    hi = a.astype(BF16)
    lo = (a - hi.astype(F32)).astype(BF16)
    return dot(hi, b, dims) + dot(lo, b, dims)


def back_kernel(
    inner, head_size, n_state, heads, share,
    tag_ref,
    ext_ref, act_ref, slope_ref, dtp_ref, join_ref, enter_ref, after_ref,
    reset_ref, weight_ref, sbias_ref, rate_ref, gain_ref, gout_ref,
    out_ref, back_ref, spill_ref, param_ref,
    dv_ref, p_ref, grad_ref, gdt_ref, dcum_ref, dsize_ref, tot_ref,
):
    length, channels = act_ref.shape
    groups, block, _ = back_ref.shape
    per = LANES // head_size
    rate = lane_row(rate_ref)
    raw, size, cum, cum_t, wgt, ent, dec, allowed, _ = token_values(
        dtp_ref[...], lane_row(sbias_ref), rate, reset_ref[...]
    )
    gain = lane_row(gain_ref)
    b_rows = act_ref[:, inner : inner + n_state]
    c_rows = act_ref[:, inner + n_state :]
    scores = dot(c_rows, b_rows, ((1,), (1,)))
    dcum_ref[...] = jnp.zeros((length, LANES), F32)
    dsize_ref[...] = jnp.zeros((length, LANES), F32)
    tot_ref[...] = jnp.zeros((16, LANES), F32)
    dscore = jnp.zeros((length, length), F32)
    db = jnp.zeros((length, n_state), F32)
    dc = jnp.zeros((length, n_state), F32)
    lane = iota((length, LANES), 1) // head_size
    row_head = iota((LANES, LANES), 0) // head_size
    col_head = iota((LANES, LANES), 1)
    dec8 = jnp.broadcast_to(dec, (8, LANES))
    gain8 = jnp.broadcast_to(gain, (8, LANES))
    for i in range(inner // LANES):
        sl = slice(i * LANES, (i + 1) * LANES)
        at, lo = divmod(i * LANES, WIDE)
        enter = enter_ref[at, :, lo : lo + LANES]
        after = after_ref[at, :, lo : lo + LANES]
        x = act_ref[:, sl].astype(F32)
        do = gout_ref[:, sl]
        do32 = do.astype(F32)
        size_b = pair(size, i, head_size, length)
        wgt_b = pair(wgt, i, head_size, length)
        ent_b = pair(ent, i, head_size, length)
        gain_b = pair(gain8, i, head_size, 8)[0:1]
        dec_b = pair(dec8, i, head_size, 8)[0:1]
        xs = (x * size_b).astype(BF16)
        xs32 = xs.astype(F32)
        within = jnp.zeros((length, LANES), F32)
        dxs = jnp.zeros((length, LANES), F32)
        for k in range(per):
            h = per * i + k
            expo = cum[:, h : h + 1] - cum_t[h : h + 1, :]
            decay = jnp.exp(jnp.where(allowed, expo, -1e30))
            mixing = (scores * decay).astype(BF16)
            mine = lane == k
            within = jnp.where(mine, dot(mixing, xs), within)
            dxs = jnp.where(mine, dot(mixing, do, ((0,), (0,))), dxs)
            dmix = dot(jnp.where(mine, do32, 0.0).astype(BF16), xs, ((1,), (1,)))
            dscore = dscore + dmix * decay
        y = within + ent_b * dot(c_rows, enter)
        out_ref[:, sl] = (y + gain_b * x).astype(BF16)
        ba = wgt_b * dot(b_rows, after)
        dxs = dxs + ba
        dv_ref[:, sl] = (dxs * size_b + gain_b * do32) * slope_ref[:, sl]
        xw = (xs32 * wgt_b).astype(BF16)
        ed = (do32 * ent_b).astype(BF16)
        db = db + dot(xw, after, ((1,), (1,)))
        dc = dc + dot(ed, enter, ((1,), (1,)))
        ind = (row_head + per * i == col_head).astype(BF16)
        dcum_ref[...] += split_dot(do32 * y - xs32 * dxs, ind)
        dsize_ref[...] += split_dot(dxs * x, ind)
        t3 = jnp.sum(xs32 * ba, axis=0, keepdims=True) + dec_b * jnp.sum(
            after.astype(F32) * enter.astype(F32), axis=0, keepdims=True
        )
        t5 = jnp.sum(do32 * x, axis=0, keepdims=True)
        both = jnp.concatenate(
            [jnp.broadcast_to(t3, (8, LANES)), jnp.broadcast_to(t5, (8, LANES))], axis=0
        )
        tot_ref[...] += split_dot(both, ind)
    dscore = dscore.astype(BF16)
    dc = dc + dot(dscore, b_rows)
    db = db + dot(dscore, c_rows, ((0,), (0,)))
    slb = slice(inner, inner + n_state)
    slc = slice(inner + n_state, channels)
    dv_ref[:, slb] = db * slope_ref[:, slb]
    dv_ref[:, slc] = dc * slope_ref[:, slc]

    t_i = iota((length, length), 0)
    s_i = iota((length, length), 1)
    is_last = iota((length, LANES), 0) == length - 1
    dcum = dcum_ref[...] + jnp.where(is_last, tot_ref[0:1, :], 0.0)
    dlog = dot((s_i >= t_i).astype(F32), dcum, precision=HIGH)
    dsize = dsize_ref[...] - dlog * rate
    draw = dsize * jax.nn.sigmoid(raw)
    gdt_ref[...] = draw
    param_ref[...] = jnp.zeros(param_ref.shape, F32)
    param_ref[0, 5:6, 0:LANES] = jnp.sum(draw, axis=0, keepdims=True)
    param_ref[0, 6:7, 0:LANES] = -jnp.sum(dlog * size, axis=0, keepdims=True)
    param_ref[0, 7:8, 0:LANES] = tot_ref[8:9, :]

    p_ref[:, 0:PAD, :] = jnp.zeros((3, PAD, LANES), F32)
    p_ref[:, PAD + length :, :] = jnp.zeros((3, PAD, LANES), F32)
    zeros = jnp.zeros((PAD, LANES), F32)
    for lo in range(0, channels, LANES):
        sl = slice(lo, lo + LANES)
        at, off = divmod(lo, share)
        col = slice(off, off + LANES)
        dv = dv_ref[:, sl]
        total = jnp.concatenate([zeros, weight_ref[3:4, sl] * dv], axis=0)
        param_ref[at, 3:4, col] = jnp.sum(dv * ext_ref[PAD:, sl], axis=0, keepdims=True)
        param_ref[at, 4:5, col] = jnp.sum(dv, axis=0, keepdims=True)
        for k in range(1, 4):
            pk = dv * join_ref[k - 1]
            p_ref[k - 1, PAD : PAD + length, :] = pk
            param_ref[at, 3 - k : 4 - k, col] = jnp.sum(
                pk * ext_ref[PAD - k : PAD - k + length, sl], axis=0, keepdims=True
            )
            total = total + weight_ref[3 - k : 4 - k, sl] * p_ref[k - 1, k : k + length + PAD, :]
        spill_ref[:, sl] = total[0:PAD].astype(BF16)
        grad_ref[:, sl] = total[PAD:]
    for g in range(groups):
        start = pl.multiple_of(tag_ref[g, 0, 0] * block, block)
        back_ref[g, :, :channels] = grad_ref[pl.ds(start, block), :].astype(BF16)
        back_ref[g, :, channels:] = gdt_ref[pl.ds(start, block), :].astype(BF16)


def return_kernel(
    n_seq, groups,
    back_ref, spill_ref, param_ref, out_ref,
    ret_ref, rspill_ref, total_ref, oout_ref,
    part, mid, fin,
    ss, rs, qss, qrs, ass, ars, bss, brs, css, crs, oss, ors,
):
    me_s, me_d = lax.axis_index("seq"), lax.axis_index("dp")
    vs, vd = home(me_s, me_d, n_seq, groups)
    after = me_s + 1 < n_seq

    for g in range(groups):
        s, d = home(me_s, g, n_seq, groups)

        @pl.when((s != me_s) | (d != me_d))
        def _():
            tell(s, d)

        @pl.when(after)
        def _():
            s1, d1 = home(me_s + 1, g, n_seq, groups)

            @pl.when((s1 != me_s) | (d1 != me_d))
            def _():
                tell(s1, d1)

    for k in range(1, n_seq):
        tell(lax.rem(me_s + k, n_seq), me_d)
    for k in range(1, groups):
        tell(me_s, lax.rem(me_d + k, groups))
    count = groups - one_if(vs == me_s) + n_seq - 1 + groups - 1
    count = count + jnp.where(vs > 0, groups - one_if(vs - 1 == me_s), 0)
    pl.semaphore_wait(pltpu.get_barrier_semaphore(), count)

    scatter = []
    for k in range(1, n_seq):
        s = lax.rem(me_s + k, n_seq)
        scatter.append(remote(param_ref.at[s], part.at[k], ass.at[k], ars.at[k], s, me_d))
    for c in scatter:
        c.start()

    def move(src, dst, ssem, rsem, s, d, act):
        mine = (s == me_s) & (d == me_d)

        @pl.when(mine)
        def _():
            act(pltpu.make_async_copy(src, dst, ssem), True)

        @pl.when(jnp.logical_not(mine))
        def _():
            act(remote(src, dst, ssem, rsem, s, d), False)

    def rows(act):
        for k in range(groups):
            j = lax.rem(me_d + k, groups)
            move(back_ref.at[j], ret_ref.at[vd], ss.at[j], rs.at[vd], vs, j, act)

    def spills(act):
        @pl.when(vs > 0)
        def _():
            for j in range(groups):
                move(spill_ref, rspill_ref.at[vd], qss.at[j], qrs.at[vd], vs - 1, j, act)

    def outs(act):
        move(out_ref, oout_ref, oss, ors, vs, vd, act)

    start = lambda c, local: c.start()
    sent = lambda c, local: c.wait() if local else c.wait_send()
    spills(start)

    @pl.when(me_s == n_seq - 1)
    def _():
        rspill_ref[...] = jnp.zeros(rspill_ref.shape, BF16)

    for c in scatter:
        c.wait()
    mine = param_ref[me_s]
    for k in range(1, n_seq):
        mine = mine + part[k]
    mid[0] = mine
    across = [
        remote(mid.at[0], mid.at[k], bss.at[k], brs.at[k], me_s, lax.rem(me_d + k, groups))
        for k in range(1, groups)
    ]
    for c in across:
        c.start()
    rows(start)
    outs(start)
    for c in across:
        c.wait()
    total = jnp.zeros(mine.shape, F32)
    for d in range(groups):
        total = total + mid[lax.rem(me_d - d + groups, groups)]
    fin[...] = total
    total_ref[me_s] = total
    gather = [
        remote(fin, total_ref.at[me_s], css.at[k], crs.at[k], lax.rem(me_s + k, n_seq), me_d)
        for k in range(1, n_seq)
    ]
    for c in gather:
        c.start()

    for g in range(groups):
        s, d = home(me_s, g, n_seq, groups)

        @pl.when((s != me_s) | (d != me_d))
        def _():
            remote(back_ref.at[g], ret_ref.at[g], ss.at[g], rs.at[g], s, d).wait_recv()

        s1, d1 = home(me_s + 1, g, n_seq, groups)

        @pl.when(after & ((s1 != me_s) | (d1 != me_d)))
        def _():
            remote(spill_ref, rspill_ref.at[g], qss.at[g], qrs.at[g], s1, d1).wait_recv()

    @pl.when((vs != me_s) | (vd != me_d))
    def _():
        remote(out_ref, oout_ref, oss, ors, vs, vd).wait_recv()

    rows(sent)
    spills(sent)
    outs(sent)
    for c in gather:
        c.wait()


def place_kernel(
    share, pack_ref, ret_ref, rspill_ref, total_ref, oout_ref,
    gin_ref, gdt_ref, gw_ref, gb_ref, gsb_ref, grate_ref, ggain_ref, out_ref, steps_ref,
):
    held, block, channels = gin_ref.shape
    heads = gdt_ref.shape[0]
    out_ref[...] = oout_ref[...]
    for j in range(held):
        g = pack_ref[0, j]
        gin_ref[j] = ret_ref[g, :, :channels]
        steps_ref[j * block : (j + 1) * block, :] = ret_ref[g, :, channels:].astype(F32)
        low = ret_ref[g, block - 2 * PAD :, :channels].astype(F32)
        extra = rspill_ref[g].astype(F32)
        last = pack_ref[1, j] == held - 1
        extra = jnp.where(last, extra, 0.0)
        gin_ref[j, block - 2 * PAD :, :] = jnp.concatenate(
            [low[:PAD], low[PAD:] + extra], axis=0
        ).astype(BF16)
    gdt_ref[...] = jnp.transpose(steps_ref[...])[:heads].astype(BF16)
    for lo in range(0, channels, LANES):
        at, off = divmod(lo, share)
        gw_ref[:, lo : lo + LANES] = total_ref[at, 0:4, off : off + LANES]
        gb_ref[lo : lo + LANES] = total_ref[at, 4, off : off + LANES]
    gsb_ref[...] = total_ref[0, 5, 0:heads]
    grate_ref[...] = total_ref[0, 6, 0:heads]
    ggain_ref[...] = total_ref[0, 7, 0:heads]


def shape(dims, kind):
    return jax.ShapeDtypeStruct(dims, kind)


def call(kernel, ins, outs, scratch=(), cid=None):
    extra = {} if cid is None else {"collective_id": cid, "has_side_effects": True}
    return pl.pallas_call(
        kernel,
        out_shape=outs,
        in_specs=ins,
        out_specs=tuple(vmem() for _ in outs),
        scratch_shapes=list(scratch),
        compiler_params=pltpu.CompilerParams(vmem_limit_bytes=VMEM_LIMIT, **extra),
    )


def per_device(
    conv_input, dt_raw, packing, resets, conv_weight, conv_bias, dt_bias, decay_rate, skip_gain, grad_out
):
    groups = lax.axis_size("dp")
    n_seq = lax.axis_size("seq")
    length, channels = conv_input.shape[1:]
    heads = dt_raw.shape[2]
    inner = grad_out.shape[2]
    head_size = inner // heads
    n_state = (channels - inner) // 2
    held = packing.shape[1]
    block = length // held
    width = channels + LANES
    pack = jnp.transpose(packing[0])
    dma = pltpu.SemaphoreType.DMA

    send, tail, tag = call(
        arrange_kernel,
        [smem(), vmem(), vmem()],
        (
            shape((groups, block, width), BF16),
            shape((groups, PAD, channels), BF16),
            shape((groups, 8, LANES), jnp.int32),
        ),
    )(pack, conv_input[0].reshape(held, block, channels), jnp.transpose(dt_raw[0]))

    got, gtag, ptail, ptag, preset, oreset, gout = call(
        functools.partial(spread_kernel, n_seq, groups),
        [vmem()] * 5,
        (
            shape((groups, block, width), BF16),
            shape((groups, 8, LANES), jnp.int32),
            shape((groups, PAD, channels), BF16),
            shape((groups, 8, LANES), jnp.int32),
            shape((1, length), jnp.int32),
            shape((1, length), jnp.int32),
            shape((length, inner), BF16),
        ),
        [dma((groups,))] * 8 + [dma((3,)), dma((3,))],
        cid=0,
    )(send, tail, tag, resets, grad_out[0])

    pieces = inner // WIDE
    state_shape = shape((pieces, n_state, WIDE), BF16)
    ext, act, slope, dtp, join, state, gstate, decay = call(
        functools.partial(front_kernel, inner, head_size, n_state),
        [smem(), smem()] + [vmem()] * 9,
        (
            shape((length + PAD, channels), F32),
            shape((length, channels), BF16),
            shape((length, channels), F32),
            shape((length, LANES), F32),
            shape((3, length, LANES), F32),
            state_shape,
            state_shape,
            shape((pieces, 8, WIDE), F32),
        ),
    )(
        gtag, ptag, got, ptail, oreset, preset, conv_weight, conv_bias, dt_bias, decay_rate, gout,
    )

    enter, after = call(
        functools.partial(chain_kernel, n_seq, groups),
        [vmem()] * 3,
        (state_shape, state_shape),
        [pltpu.VMEM(state_shape.shape, BF16)] * 4 + [dma((pieces,))] * 4,
        cid=1,
    )(state, gstate, decay)

    tiles = channels // LANES
    share = -(-tiles // n_seq) * LANES
    params = shape((n_seq, 8, share), F32)
    out, back, spill, param = call(
        functools.partial(back_kernel, inner, head_size, n_state, heads, share),
        [smem()] + [vmem()] * 13,
        (
            shape((length, inner), BF16),
            shape((groups, block, width), BF16),
            shape((PAD, channels), BF16),
            params,
        ),
        [
            pltpu.VMEM((length, channels), F32),
            pltpu.VMEM((3, length + 2 * PAD, LANES), F32),
            pltpu.VMEM((length, channels), F32),
            pltpu.VMEM((length, LANES), F32),
            pltpu.VMEM((length, LANES), F32),
            pltpu.VMEM((length, LANES), F32),
            pltpu.VMEM((16, LANES), F32),
        ],
    )(
        gtag, ext, act, slope, dtp, join, enter, after, oreset, conv_weight, dt_bias, decay_rate,
        skip_gain, gout,
    )

    ret, rspill, total, oout = call(
        functools.partial(return_kernel, n_seq, groups),
        [vmem()] * 4,
        (
            shape((groups, block, width), BF16),
            shape((groups, PAD, channels), BF16),
            params,
            shape((length, inner), BF16),
        ),
        [
            pltpu.VMEM((n_seq, 8, share), F32),
            pltpu.VMEM((groups, 8, share), F32),
            pltpu.VMEM((8, share), F32),
        ]
        + [dma((groups,))] * 4
        + [dma((n_seq,))] * 2
        + [dma((groups,))] * 2
        + [dma((n_seq,))] * 2
        + [dma, dma],
        cid=2,
    )(back, spill, param, out)

    gin, gdt, gw, gb, gsb, grate, ggain, layer_out = call(
        functools.partial(place_kernel, share),
        [smem()] + [vmem()] * 4,
        (
            shape((held, block, channels), BF16),
            shape((heads, length), BF16),
            shape((4, channels), F32),
            shape((channels,), F32),
            shape((heads,), F32),
            shape((heads,), F32),
            shape((heads,), F32),
            shape((length, inner), BF16),
        ),
        [pltpu.VMEM((length, LANES), F32)],
    )(pack, ret, rspill, total, oout)
    return (
        layer_out[None],
        gin.reshape(1, length, channels),
        jnp.transpose(gdt)[None],
        gw,
        gb,
        gsb,
        grate,
        ggain,
    )


def solution(mesh):
    tokens = P("dp", "seq", None)
    in_specs = (tokens, tokens, tokens, P("dp", "seq"), P(), P(), P(), P(), P(), tokens)
    out_specs = (tokens, tokens, tokens, P(), P(), P(), P(), P())
    return jax.shard_map(
        per_device, mesh=mesh, in_specs=in_specs, out_specs=out_specs, check_vma=False
    )
```
